32 devices in a mesh: rep: 2 (over x), ep: 16 (over z, y, core).
Axes of the slice: x: 2, y: 2, z: 4, core: 2. Of those that a mesh axis runs over, the one named last changes fastest.
Arguments:
- tokens: bfloat16 [128, 2048], P('ep'), may hold values from -6 to 6
- cotangent: bfloat16 [128, 2048], P('ep'), may hold values from -4 to 4
- expert_ids: int32 [128, 8], P('ep'), may hold values from 0 to 15, as said below
- route_weights: float32 [128, 8], P('ep'), may hold values from 0.1 to 0.6
- helper: int32 [16], replicated, may hold values from 0 to 15, as said below
- gate_weight: bfloat16 [16, 2048, 768], P('ep', None, 'rep'), may hold values from -0.125 to 0.125
- up_weight: bfloat16 [16, 2048, 768], P('ep', None, 'rep'), may hold values from -0.125 to 0.125
- down_weight: bfloat16 [16, 768, 2048], P('ep', 'rep'), may hold values from -0.21875 to 0.21875
Outputs:
- mixed: bfloat16 [128, 2048], P('ep')
- grad_tokens: bfloat16 [128, 2048], P('ep')
- grad_gate: bfloat16 [16, 2048, 768], P('ep', None, 'rep')
- grad_up: bfloat16 [16, 2048, 768], P('ep', None, 'rep')
- grad_down: bfloat16 [16, 768, 2048], P('ep', 'rep')
The draws below stay inside these ranges and needn't reach their ends.
Inputs may be any that keep to these rules, and one draw needn't show every extreme that they name: `expert_ids`: each token names 8 different experts. helper[e] is e or (e + 8) mod 16. Exactly 2 experts have helper[e] != e, and for them helper[helper[e]] == helper[e].
All inputs are finite; a program needn't handle non-finite values.
Results may differ from the reference program's by a relative error of at most 0.012.
Values may be sent and summed in bfloat16 or wider, within the bound.
No kernel may reach another device: no remote copies, remote signals or barrier semaphores. Data moves between devices by JAX's collectives and lax.ppermute only.
A program may use at most 128 MiB of HBM per device.

```python
import jax
import jax.numpy as jnp
from jax import lax

D = 2048
FF = 768
TOP = 8
EXPERTS = 16
TOK_DEV = 8
TOKENS = 128
CAP_HOME = 4
SPARE = 2
HOT_CAP = 6
HELPER_CAP = 2
N_REP = 2


def hot_pairs(key):
    half_count = EXPERTS // 2
    chosen = jax.random.permutation(jax.random.fold_in(key, 101), half_count)[:EXPERTS // 8]
    side_bits = jax.random.randint(jax.random.fold_in(key, 102), (EXPERTS // 8,), 0, 2)
    hot_ids = (chosen + side_bits * half_count).astype(jnp.int32)
    return jnp.zeros((EXPERTS,), jnp.int32).at[hot_ids].set(1)


def draw_helper(key, part):
    hot_mask = hot_pairs(key)
    expert_index = jnp.arange(EXPERTS, dtype=jnp.int32)
    return jnp.where(hot_mask > 0, (expert_index + EXPERTS // 2) % EXPERTS, expert_index).astype(jnp.int32)


def block_counts(block_key, hot_mask):
    expert_index = jnp.arange(EXPERTS, dtype=jnp.int32)
    lending_mask = hot_mask[(expert_index + EXPERTS // 2) % EXPERTS]
    base_count = jnp.where(hot_mask > 0, HOT_CAP, jnp.where(lending_mask > 0, HELPER_CAP, CAP_HOME)).astype(jnp.int32)
    pair_order = jax.random.permutation(jax.random.fold_in(block_key, 4), EXPERTS)
    shift_size = jax.random.randint(jax.random.fold_in(block_key, 5), (EXPERTS // 2,), 0, SPARE + 1)
    sign_bits = 2 * jax.random.randint(jax.random.fold_in(block_key, 6), (EXPERTS // 2,), 0, 2) - 1
    paired = jnp.stack((shift_size * sign_bits, -shift_size * sign_bits), axis=1).reshape(EXPERTS)
    deltas = jnp.zeros((EXPERTS,), jnp.int32).at[pair_order].set(paired.astype(jnp.int32))
    return (base_count + deltas).astype(jnp.int32)


def source_block(block_key, hot_mask):
    counts = block_counts(block_key, hot_mask)
    expert_order = jax.random.permutation(jax.random.fold_in(block_key, 1), EXPERTS).astype(jnp.int32)
    run_ends = jnp.cumsum(counts[expert_order])
    positions = jnp.arange(TOK_DEV * TOP, dtype=jnp.int32)
    bucket_index = jnp.sum((run_ends[None, :] <= positions[:, None]).astype(jnp.int32), axis=1)
    listed = expert_order[bucket_index]
    block_ids = listed.reshape(TOP, TOK_DEV).T
    token_order = jax.random.permutation(jax.random.fold_in(block_key, 2), TOK_DEV)
    block_ids = block_ids[token_order]
    slot_keys = jax.random.split(jax.random.fold_in(block_key, 3), TOK_DEV)
    slot_orders = jax.vmap(lambda one_key: jax.random.permutation(one_key, TOP))(slot_keys)
    return jnp.take_along_axis(block_ids, slot_orders, axis=1).astype(jnp.int32)


def draw_expert_ids(key, part):
    hot_mask = hot_pairs(key)
    block_keys = jax.random.split(jax.random.fold_in(key, 103), EXPERTS)
    blocks = jax.vmap(lambda block_key: source_block(block_key, hot_mask))(block_keys)
    return blocks.reshape(EXPERTS * TOK_DEV, TOP).astype(jnp.int32)


def block_levels(own_key, dims, shards, least, high):
    def one(axis_at, shards_of):
        heights = jax.random.uniform(jax.random.fold_in(jax.random.fold_in(own_key, 6), axis_at), (shards_of,), jnp.float32, least / len(shards), high / len(shards))
        return jnp.repeat(jnp.exp(heights), dims[axis_at] // shards_of).reshape((-1,) + (1,) * (len(dims) - axis_at - 1))

    factor_of = one(*shards[0])
    for cut in shards[1:]:
        factor_of = factor_of * one(*cut)
    return factor_of


def scatter_about(rng, extent, scale, most, cuts=(), kind=jnp.bfloat16):
    array = jax.random.normal(rng, extent, jnp.float32) * scale
    if len(cuts) > 0:
        array = block_levels(rng, extent, cuts, -0.22, 0.18) * array
    return jnp.clip(array, min=-most, max=most).astype(kind)


def setup_inputs(seed: int = 0) -> dict:
    key_of = jax.random.split(jax.random.key(seed), 9)
    tokens = scatter_about(key_of[0], (TOKENS, D), 1.0, 6.0, ((0, 16),))
    cotangent = scatter_about(key_of[1], (TOKENS, D), 0.5, 4.0, ((0, 16),))
    expert_ids = draw_expert_ids(jax.random.fold_in(key_of[8], 71), 0)
    route_weights = jnp.clip(0.1 + 0.5 * jax.random.uniform(key_of[3], (TOKENS, TOP), jnp.float32) ** block_levels(key_of[3], (TOKENS, TOP), ((0, 16),), -0.2, 0.2), 0.1, 0.6)
    helper = draw_helper(jax.random.fold_in(key_of[8], 71), 0)
    gate_weight = scatter_about(key_of[5], (EXPERTS, D, FF), D ** -0.5, 0.125, ((0, 16), (2, 2)))
    up_weight = scatter_about(key_of[6], (EXPERTS, D, FF), D ** -0.5, 0.125, ((0, 16), (2, 2)))
    down_weight = scatter_about(key_of[7], (EXPERTS, FF, D), FF ** -0.5, 0.21875, ((0, 16), (1, 2)))
    return dict(tokens=tokens, cotangent=cotangent, expert_ids=expert_ids, route_weights=route_weights, helper=helper, gate_weight=gate_weight, up_weight=up_weight, down_weight=down_weight)


def fold_rounded(partial_sum):
    return lax.optimization_barrier(partial_sum.astype(jnp.bfloat16)).astype(jnp.float32)


def expert_pass(rows_in, rows_grad, gate_matrix, up_matrix, down_matrix):
    gate_pre = jnp.dot(rows_in, gate_matrix, preferred_element_type=jnp.float32)
    up_pre = jnp.dot(rows_in, up_matrix, preferred_element_type=jnp.float32)
    sigmoid_gate = jax.nn.sigmoid(gate_pre)
    hidden = (gate_pre * sigmoid_gate * up_pre).astype(jnp.bfloat16)
    d_hidden = jnp.dot(rows_grad, down_matrix.T, preferred_element_type=jnp.float32)
    d_gate = (d_hidden * up_pre * sigmoid_gate * (1.0 + gate_pre * (1.0 - sigmoid_gate))).astype(jnp.bfloat16)
    d_up = (d_hidden * gate_pre * sigmoid_gate).astype(jnp.bfloat16)
    section_width = gate_matrix.shape[1] // N_REP
    out_rows = jnp.zeros((rows_in.shape[0], down_matrix.shape[1]), jnp.float32)
    back_rows = jnp.zeros((rows_in.shape[0], gate_matrix.shape[0]), jnp.float32)
    for section in range(N_REP):
        col_start = section * section_width
        col_end = col_start + section_width
        out_part = jnp.dot(hidden[:, col_start:col_end], down_matrix[col_start:col_end], preferred_element_type=jnp.float32)
        back_part = jnp.dot(d_gate[:, col_start:col_end], gate_matrix[:, col_start:col_end].T, preferred_element_type=jnp.float32)
        back_part = back_part + jnp.dot(d_up[:, col_start:col_end], up_matrix[:, col_start:col_end].T, preferred_element_type=jnp.float32)
        out_rows = out_rows + fold_rounded(out_part)
        back_rows = back_rows + fold_rounded(back_part)
    grad_gate = jnp.dot(rows_in.T, d_gate, preferred_element_type=jnp.float32)
    grad_up = jnp.dot(rows_in.T, d_up, preferred_element_type=jnp.float32)
    grad_down = jnp.dot(hidden.T, rows_grad, preferred_element_type=jnp.float32)
    return out_rows.astype(jnp.bfloat16), back_rows.astype(jnp.bfloat16), (grad_gate, grad_up, grad_down)


def expert_limits(helper):
    expert_index = jnp.arange(EXPERTS, dtype=jnp.int32)
    hot_flags = (helper != expert_index).astype(jnp.int32)
    lending_flags = jnp.roll(hot_flags, EXPERTS // 2)
    limits = jnp.where(hot_flags > 0, HOT_CAP, jnp.where(lending_flags > 0, HELPER_CAP, CAP_HOME)).astype(jnp.int32)
    return hot_flags, limits


def slot_table(expert_ids, helper):
    tok_count = expert_ids.shape[0] // EXPERTS
    block_ids = expert_ids.reshape(EXPERTS, tok_count * TOP)
    expert_index = jnp.arange(EXPERTS, dtype=jnp.int32)
    onehot = (block_ids[:, :, None] == expert_index[None, None, :]).astype(jnp.int32)
    pair_ranks = jnp.sum((jnp.cumsum(onehot, axis=1) - onehot) * onehot, axis=2).astype(jnp.int32)
    hot_flags, limits = expert_limits(helper)
    retained = pair_ranks < limits[block_ids]
    source_index = expert_index[:, None]
    position = block_ids * (EXPERTS * HOT_CAP) + source_index * HOT_CAP + pair_ranks
    position = jnp.where(retained, position, EXPERTS * EXPERTS * HOT_CAP).astype(jnp.int32)
    pair_index = jnp.arange(EXPERTS * tok_count * TOP, dtype=jnp.int32)
    pair_table = jnp.full((EXPERTS * EXPERTS * HOT_CAP,), -1, jnp.int32)
    pair_table = pair_table.at[position.reshape(-1)].set(pair_index, mode="drop")
    return pair_table.reshape(EXPERTS, EXPERTS, HOT_CAP), hot_flags


def reference(tokens, cotangent, expert_ids, route_weights, helper, gate_weight, up_weight, down_weight):
    pair_table, hot_flags = slot_table(expert_ids, helper)
    flat_weights = route_weights.reshape(-1)
    expert_order = jnp.argsort(hot_flags, stable=True).astype(jnp.int32)
    cold_count = EXPERTS - EXPERTS // 8
    cold_ids = expert_order[:cold_count]
    hot_ids = expert_order[cold_count:]
    cold_table = pair_table[cold_ids][:, :, :CAP_HOME].reshape(cold_count, EXPERTS * CAP_HOME)
    hot_table = pair_table[hot_ids].reshape(EXPERTS - cold_count, EXPERTS * HOT_CAP)

    def one_expert(carried, inputs):
        mixed_acc, back_acc = carried
        slot_pairs, expert_id = inputs
        filled = slot_pairs >= 0
        pair_safe = jnp.maximum(slot_pairs, 0).astype(jnp.int32)
        token_safe = (pair_safe // TOP).astype(jnp.int32)
        rows_in = jnp.where(filled[:, None], tokens[token_safe], jnp.zeros((), jnp.bfloat16))
        weight_rows = jnp.where(filled, flat_weights[pair_safe], jnp.zeros((), jnp.float32))
        rows_grad = (weight_rows[:, None] * cotangent[token_safe].astype(jnp.float32)).astype(jnp.bfloat16)
        out_rows, back_rows, grad_parts = expert_pass(rows_in, rows_grad, gate_weight[expert_id], up_weight[expert_id], down_weight[expert_id])
        mixed_acc = mixed_acc.at[token_safe].add(weight_rows[:, None] * out_rows.astype(jnp.float32))
        back_acc = back_acc.at[token_safe].add(jnp.where(filled[:, None], back_rows.astype(jnp.float32), jnp.zeros((), jnp.float32)))
        rounded = (grad_parts[0].astype(jnp.bfloat16), grad_parts[1].astype(jnp.bfloat16), grad_parts[2].astype(jnp.bfloat16))
        return (mixed_acc, back_acc), rounded

    start_acc = jnp.zeros(tokens.shape, jnp.float32)
    carried, cold_grads = lax.scan(one_expert, (start_acc, start_acc), (cold_table, cold_ids))
    carried, hot_grads = lax.scan(one_expert, carried, (hot_table, hot_ids))
    mixed_acc, back_acc = carried
    grad_gate = jnp.zeros(gate_weight.shape, jnp.bfloat16).at[cold_ids].set(cold_grads[0]).at[hot_ids].set(hot_grads[0])
    grad_up = jnp.zeros(up_weight.shape, jnp.bfloat16).at[cold_ids].set(cold_grads[1]).at[hot_ids].set(hot_grads[1])
    grad_down = jnp.zeros(down_weight.shape, jnp.bfloat16).at[cold_ids].set(cold_grads[2]).at[hot_ids].set(hot_grads[2])
    return mixed_acc.astype(jnp.bfloat16), back_acc.astype(jnp.bfloat16), grad_gate, grad_up, grad_down
```

```python
import functools

import jax
import jax.numpy as jnp
from jax import lax
from jax.experimental import pallas as pl
from jax.experimental.pallas import tpu as pltpu
from jax.sharding import PartitionSpec as P

TOP = 8
CAP_HOME = 4
HOT_CAP = 6
HELPER_CAP = 2

LANES = 128
VMEM_SPEC = pl.BlockSpec(memory_space=pltpu.VMEM)
SMEM_SPEC = pl.BlockSpec(memory_space=pltpu.SMEM)
F32 = jnp.float32
BF16 = jnp.bfloat16


def dot_nn(a, b):
    return jnp.dot(a, b, preferred_element_type=F32)


def dot_nt(a, b):
    return lax.dot_general(a, b, (((1,), (1,)), ((), ())), preferred_element_type=F32)


def dot_tn(a, b):
    return lax.dot_general(a, b, (((0,), (0,)), ((), ())), preferred_element_type=F32)


def pack_kernel(tokens_ref, cotangent_ref, ids_ref, weights_ref, out_ref):
    rows, width = tokens_ref.shape
    both = jnp.concatenate([tokens_ref[...].astype(F32), cotangent_ref[...].astype(F32)], axis=0)
    out_ref[:, :width] = both.astype(BF16)
    weights = weights_ref[...]
    first = weights.astype(BF16).astype(F32)
    rest = weights - first
    second = rest.astype(BF16).astype(F32)
    third = rest - second
    lane = lax.broadcasted_iota(jnp.int32, (TOP, LANES), 1)
    row = lax.broadcasted_iota(jnp.int32, (TOP, LANES), 0)
    place_low = (lane == row).astype(F32).astype(BF16)
    place_high = (lane == row + TOP).astype(F32).astype(BF16)
    token_side = dot_nn(ids_ref[...].astype(F32).astype(BF16), place_low) + dot_nn(
        first.astype(BF16), place_high
    )
    grad_side = dot_nn(second.astype(BF16), place_low) + dot_nn(third.astype(BF16), place_high)
    out_ref[:, width:] = jnp.concatenate([token_side, grad_side], axis=0).astype(BF16)


def expert_kernel(chips, *refs):
    place_ref, helper_ref = refs[:2]
    own_refs = refs[2 : 2 + chips]
    other_refs = refs[2 + chips : 2 + 2 * chips]
    gate_ref, up_ref, down_ref = refs[2 + 2 * chips : 5 + 2 * chips]
    keep_ref, give_ref, rows_ref, scaled_ref, hidden_ref, dgate_ref, dup_ref = refs[5 + 2 * chips : 12 + 2 * chips]
    cot_ref, aux_ref = refs[12 + 2 * chips :]
    expert = place_ref[0]
    is_low = place_ref[1] == 0
    width = rows_ref.shape[1]
    block = own_refs[0].shape[0] // 2
    pair = 2 * block
    total = chips * pair
    experts = 2 * chips

    for chip in range(chips):
        mine = own_refs[chip][...].astype(F32)
        theirs = other_refs[chip][...].astype(F32)
        low = jnp.where(is_low, mine, theirs)
        high = jnp.where(is_low, theirs, mine)
        token_rows = jnp.concatenate([low[:block], high[:block]], axis=0)
        grad_rows = jnp.concatenate([low[block:], high[block:]], axis=0)
        span = slice(chip * pair, (chip + 1) * pair)
        rows_ref[span, :] = token_rows[:, :width].astype(BF16)
        cot_ref[span, :] = grad_rows[:, :width].astype(BF16)
        aux_ref[0, span, :] = token_rows[:, width:]
        aux_ref[1, span, :] = grad_rows[:, width:]

    def lends(index, found):
        here = helper_ref[index]
        return found | ((here != index) & (here == expert)).astype(jnp.int32)

    lending = lax.fori_loop(0, experts, lends, jnp.int32(0))
    hot = helper_ref[expert] != expert
    limit = jnp.where(hot, HOT_CAP, jnp.where(lending > 0, HELPER_CAP, CAP_HOME)).astype(F32)

    token_side = aux_ref[0]
    grad_side = aux_ref[1]
    lane = lax.broadcasted_iota(jnp.int32, (total, LANES), 1)
    match = jnp.where((lane < TOP) & (token_side == expert.astype(F32)), 1.0, 0.0)
    shifted = pltpu.roll(match, TOP, 1)
    weight = jnp.sum(match * grad_side + shifted * (token_side + grad_side), axis=1, keepdims=True)
    row_at = lax.broadcasted_iota(jnp.int32, (total, total), 0)
    col_at = lax.broadcasted_iota(jnp.int32, (total, total), 1)
    earlier = jnp.where((row_at // block == col_at // block) & (col_at < row_at), 1.0, 0.0)
    rank = jnp.sum(dot_nn(earlier.astype(BF16), match.astype(BF16)), axis=1, keepdims=True)
    weight = jnp.where(rank < limit, weight, 0.0)

    rows = rows_ref[...]
    gate = gate_ref[0]
    up = up_ref[0]
    down = down_ref[0]
    scaled = (weight * cot_ref[...].astype(F32)).astype(BF16)
    scaled_ref[...] = scaled
    gate_pre = dot_nn(rows, gate)
    up_pre = dot_nn(rows, up)
    d_hidden = dot_nt(scaled, down)
    sigmoid_gate = jax.nn.sigmoid(gate_pre)
    hidden = (gate_pre * sigmoid_gate * up_pre).astype(BF16)
    d_gate = (d_hidden * up_pre * sigmoid_gate * (1.0 + gate_pre * (1.0 - sigmoid_gate))).astype(BF16)
    d_up = (d_hidden * gate_pre * sigmoid_gate).astype(BF16)
    hidden_ref[...] = hidden
    dgate_ref[...] = d_gate
    dup_ref[...] = d_up
    out_part = weight * dot_nn(hidden, down)
    back_part = dot_nt(d_gate, gate) + dot_nt(d_up, up)
    keep_ref[...] = jnp.where(is_low, out_part, back_part)
    give_ref[...] = jnp.where(is_low, back_part, out_part).astype(BF16)


def grads_kernel(rows_ref, scaled_ref, hidden_ref, dgate_ref, dup_ref, gate_out, up_out, down_out):
    rows = rows_ref[...]
    gate_out[0] = dot_tn(rows, dgate_ref[...]).astype(BF16)
    up_out[0] = dot_tn(rows, dup_ref[...]).astype(BF16)
    down_out[0] = dot_tn(hidden_ref[...], scaled_ref[...]).astype(BF16)


def chip_sum_kernel(keep_ref, got_ref, *out_refs):
    pair = out_refs[0].shape[0]
    for chip, out_ref in enumerate(out_refs):
        span = slice(chip * pair, (chip + 1) * pair)
        out_ref[...] = (keep_ref[span, :] + got_ref[span, :].astype(F32)).astype(BF16)


def plane_sum_kernel(place_ref, *refs):
    part_refs, (mine_ref, other_ref) = refs[:-2], refs[-2:]
    total = part_refs[0][...].astype(F32)
    for part_ref in part_refs[1:]:
        total = total + part_ref[...].astype(F32)
    block = mine_ref.shape[0]
    is_low = place_ref[1] == 0
    low, high = total[:block], total[block:]
    mine_ref[...] = jnp.where(is_low, low, high).astype(BF16)
    other_ref[...] = jnp.where(is_low, high, low).astype(BF16)


def last_sum_kernel(place_ref, mine_ref, across_ref, beside_ref, corner_ref, mixed_ref, grad_ref):
    is_low = place_ref[1] == 0
    own_array = mine_ref[...].astype(F32) + across_ref[...].astype(F32)
    other_array = beside_ref[...].astype(F32) + corner_ref[...].astype(F32)
    mixed_ref[...] = jnp.where(is_low, own_array, other_array).astype(BF16)
    grad_ref[...] = jnp.where(is_low, other_array, own_array).astype(BF16)


def dense_local(
    tokens, cotangent, expert_ids, route_weights, helper, gate_weight, up_weight, down_weight
):
    experts = lax.axis_size("ep")
    chips = experts // 2
    block, width = tokens.shape
    hidden_width = gate_weight.shape[2]
    place_index = lax.axis_index("ep").astype(jnp.int32)
    place = jnp.stack([place_index, place_index % 2])

    def over_ep(value, offset):
        return lax.ppermute(value, "ep", [(at, at ^ offset) for at in range(experts)])

    def over_all(value, flip_rep, flip_core):
        pairs = [
            (rep * experts + at, (rep ^ flip_rep) * experts + (at ^ flip_core))
            for rep in range(2)
            for at in range(experts)
        ]
        return lax.ppermute(value, ("rep", "ep"), pairs)

    packed = pl.pallas_call(
        pack_kernel,
        out_shape=jax.ShapeDtypeStruct((2 * block, width + LANES), BF16),
        in_specs=[VMEM_SPEC] * 4,
        out_specs=VMEM_SPEC,
        name="pack_rows",
    )(tokens, cotangent, expert_ids, route_weights)
    own = [packed] + [None] * (chips - 1)
    for chip in range(chips - 1, 0, -1):
        own[chip] = over_ep(packed, 2 * chip)
    other = [over_ep(part, 1) for part in own]

    total = 2 * block * chips
    keep, give, rows, scaled, hidden, d_gate, d_up = pl.pallas_call(
        functools.partial(expert_kernel, chips),
        out_shape=(
            jax.ShapeDtypeStruct((total, width), F32),
            jax.ShapeDtypeStruct((total, width), BF16),
            jax.ShapeDtypeStruct((total, width), BF16),
            jax.ShapeDtypeStruct((total, width), BF16),
            jax.ShapeDtypeStruct((total, hidden_width), BF16),
            jax.ShapeDtypeStruct((total, hidden_width), BF16),
            jax.ShapeDtypeStruct((total, hidden_width), BF16),
        ),
        in_specs=[SMEM_SPEC] * 2 + [VMEM_SPEC] * (2 * chips + 3),
        out_specs=[VMEM_SPEC] * 7,
        scratch_shapes=[pltpu.VMEM((total, width), BF16), pltpu.VMEM((2, total, LANES), F32)],
        name="expert_rows",
    )(place, helper, *own, *other, gate_weight, up_weight, down_weight)

    got = over_ep(give, 1)
    parts = pl.pallas_call(
        chip_sum_kernel,
        out_shape=[jax.ShapeDtypeStruct((2 * block, width), BF16)] * chips,
        in_specs=[VMEM_SPEC] * 2,
        out_specs=[VMEM_SPEC] * chips,
        name="chip_sum",
    )(keep, got)
    arrived = [parts[0]] + [over_ep(parts[chip], 2 * chip) for chip in range(chips - 1, 0, -1)]

    steps = 4
    column = width // steps
    grad_gate, grad_up, grad_down = pl.pallas_call(
        grads_kernel,
        grid=(steps,),
        out_shape=(
            jax.ShapeDtypeStruct((1, width, hidden_width), BF16),
            jax.ShapeDtypeStruct((1, width, hidden_width), BF16),
            jax.ShapeDtypeStruct((1, hidden_width, width), BF16),
        ),
        in_specs=[
            pl.BlockSpec((total, column), lambda step: (0, step)),
            pl.BlockSpec((total, column), lambda step: (0, step)),
            pl.BlockSpec((total, hidden_width), lambda step: (0, 0)),
            pl.BlockSpec((total, hidden_width), lambda step: (0, 0)),
            pl.BlockSpec((total, hidden_width), lambda step: (0, 0)),
        ],
        out_specs=(
            pl.BlockSpec((1, column, hidden_width), lambda step: (0, step, 0)),
            pl.BlockSpec((1, column, hidden_width), lambda step: (0, step, 0)),
            pl.BlockSpec((1, hidden_width, column), lambda step: (0, 0, step)),
        ),
        name="weight_grads",
    )(rows, scaled, hidden, d_gate, d_up)

    mine, theirs = pl.pallas_call(
        plane_sum_kernel,
        out_shape=[jax.ShapeDtypeStruct((block, width), BF16)] * 2,
        in_specs=[SMEM_SPEC] + [VMEM_SPEC] * chips,
        out_specs=[VMEM_SPEC] * 2,
        name="plane_sum",
    )(place, *arrived)
    corner = over_all(theirs, 1, 1)
    across = over_all(mine, 1, 0)
    beside = over_all(theirs, 0, 1)
    mixed, grad_tokens = pl.pallas_call(
        last_sum_kernel,
        out_shape=[jax.ShapeDtypeStruct((block, width), BF16)] * 2,
        in_specs=[SMEM_SPEC] + [VMEM_SPEC] * 4,
        out_specs=[VMEM_SPEC] * 2,
        name="last_sum",
    )(place, mine, across, beside, corner)
    return mixed, grad_tokens, grad_gate, grad_up, grad_down


def few_tokens(mesh_shape, token_count):
    experts = mesh_shape["ep"]
    block = token_count // experts
    return (
        mesh_shape["rep"] == 2
        and experts >= 4
        and experts & (experts - 1) == 0
        and experts <= 256
        and block == 8
        and block <= 2 * HOT_CAP
    )


def local(*args):
    sizes = {"rep": lax.axis_size("rep"), "ep": lax.axis_size("ep")}
    if few_tokens(sizes, args[0].shape[0] * sizes["ep"]):
        return dense_local(*args)
    return slot_local(*args)


def swiglu_pass(rows_in, rows_grad, gate_matrix, up_matrix, down_matrix):
    gate_pre = jnp.dot(rows_in, gate_matrix, preferred_element_type=jnp.float32)
    up_pre = jnp.dot(rows_in, up_matrix, preferred_element_type=jnp.float32)
    sigmoid_gate = jax.nn.sigmoid(gate_pre)
    hidden = (gate_pre * sigmoid_gate * up_pre).astype(jnp.bfloat16)
    out_part = jnp.dot(hidden, down_matrix, preferred_element_type=jnp.float32)
    d_hidden = lax.dot_general(
        rows_grad, down_matrix, (((1,), (1,)), ((), ())), preferred_element_type=jnp.float32
    )
    d_gate = (d_hidden * up_pre * sigmoid_gate * (1.0 + gate_pre * (1.0 - sigmoid_gate))).astype(
        jnp.bfloat16
    )
    d_up = (d_hidden * gate_pre * sigmoid_gate).astype(jnp.bfloat16)
    back_part = lax.dot_general(
        d_gate, gate_matrix, (((1,), (1,)), ((), ())), preferred_element_type=jnp.float32
    )
    back_part = back_part + lax.dot_general(
        d_up, up_matrix, (((1,), (1,)), ((), ())), preferred_element_type=jnp.float32
    )
    grad_gate = lax.dot_general(
        rows_in, d_gate, (((0,), (0,)), ((), ())), preferred_element_type=jnp.float32
    )
    grad_up = lax.dot_general(
        rows_in, d_up, (((0,), (0,)), ((), ())), preferred_element_type=jnp.float32
    )
    grad_down = lax.dot_general(
        hidden, rows_grad, (((0,), (0,)), ((), ())), preferred_element_type=jnp.float32
    )
    return (out_part, back_part, grad_gate, grad_up, grad_down)


def slot_local(
    tokens, cotangent, expert_ids, route_weights, helper, gate_weight, up_weight, down_weight
):
    experts = lax.axis_size("ep")
    half_axis = experts // 2
    tok_count = tokens.shape[0]
    feature_width = tokens.shape[1]
    pair_count = tok_count * TOP
    flat_ids = expert_ids.reshape(pair_count)
    expert_index = jnp.arange(experts, dtype=jnp.int32)
    onehot = (flat_ids[:, None] == expert_index[None, :]).astype(jnp.int32)
    pair_ranks = jnp.sum((jnp.cumsum(onehot, axis=0) - onehot) * onehot, axis=1)
    hot_flags = (helper != expert_index).astype(jnp.int32)
    lending_flags = jnp.roll(hot_flags, half_axis)
    limits = jnp.where(
        hot_flags > 0, HOT_CAP, jnp.where(lending_flags > 0, HELPER_CAP, CAP_HOME)
    ).astype(jnp.int32)
    pair_limit = jnp.sum(onehot * limits[None, :], axis=1)
    retained = pair_ranks < pair_limit
    slot_width = HOT_CAP
    slot_count = experts * slot_width
    slot_index = jnp.where(retained, flat_ids * slot_width + pair_ranks, slot_count)
    pair_index = jnp.arange(pair_count, dtype=jnp.int32)
    slot_pairs = jnp.full((slot_count,), -1, jnp.int32).at[slot_index].set(pair_index, mode="drop")
    filled = slot_pairs >= 0
    pair_safe = jnp.maximum(slot_pairs, 0)
    token_safe = pair_safe // TOP
    send_in = jnp.where(filled[:, None], tokens[token_safe], jnp.zeros((), jnp.bfloat16))
    slot_weight = jnp.where(
        filled, route_weights.reshape(pair_count)[pair_safe], jnp.zeros((), jnp.float32)
    )
    send_grad = (slot_weight[:, None] * cotangent[token_safe].astype(jnp.float32)).astype(
        jnp.bfloat16
    )
    send_in = send_in.reshape(experts, slot_width, feature_width)
    send_grad = send_grad.reshape(experts, slot_width, feature_width)
    half_slots = slot_width // lax.axis_size("rep")
    slot_start = lax.axis_index("rep") * half_slots
    part_in = lax.dynamic_slice_in_dim(send_in, slot_start, half_slots, 1)
    part_grad = lax.dynamic_slice_in_dim(send_grad, slot_start, half_slots, 1)
    got_in, got_grad = (
        lax.all_to_all(part_in, "ep", split_axis=0, concat_axis=0, tiled=True),
        lax.all_to_all(part_grad, "ep", split_axis=0, concat_axis=0, tiled=True),
    )
    received_in, received_grad = (
        lax.all_gather(got_in, "rep", axis=1, tiled=True),
        lax.all_gather(got_grad, "rep", axis=1, tiled=True),
    )
    own_gate = gate_weight[0]
    own_up = up_weight[0]
    own_down = down_weight[0]
    out_flat, back_flat, total_gate, total_up, total_down = swiglu_pass(
        received_in.reshape(-1, feature_width),
        received_grad.reshape(-1, feature_width),
        own_gate,
        own_up,
        own_down,
    )
    out_part = out_flat.reshape(experts, slot_width, feature_width)
    back_part = back_flat.reshape(experts, slot_width, feature_width)
    out_sum, back_sum = (
        lax.psum_scatter(
            out_part.astype(jnp.bfloat16), "rep", scatter_dimension=1, tiled=True
        ).astype(jnp.float32),
        lax.psum_scatter(
            back_part.astype(jnp.bfloat16), "rep", scatter_dimension=1, tiled=True
        ).astype(jnp.float32),
    )
    got_out, got_back = (
        lax.all_to_all(out_sum.astype(jnp.bfloat16), "ep", split_axis=0, concat_axis=0, tiled=True),
        lax.all_to_all(
            back_sum.astype(jnp.bfloat16), "ep", split_axis=0, concat_axis=0, tiled=True
        ),
    )
    out_rows, back_rows = (
        lax.all_gather(got_out, "rep", axis=1, tiled=True),
        lax.all_gather(got_back, "rep", axis=1, tiled=True),
    )
    out_table = out_rows.reshape(slot_count, feature_width)
    back_table = back_rows.reshape(slot_count, feature_width)
    pair_slot = jnp.where(retained, slot_index, 0)
    picked_out = jnp.where(retained[:, None], out_table[pair_slot], jnp.zeros((), jnp.bfloat16))
    picked_back = jnp.where(retained[:, None], back_table[pair_slot], jnp.zeros((), jnp.bfloat16))
    mixed = jnp.sum(
        route_weights[:, :, None]
        * picked_out.astype(jnp.float32).reshape(tok_count, TOP, feature_width),
        axis=1,
    ).astype(jnp.bfloat16)
    grad_tokens = jnp.sum(
        picked_back.astype(jnp.float32).reshape(tok_count, TOP, feature_width), axis=1
    ).astype(jnp.bfloat16)
    return (
        mixed,
        grad_tokens,
        total_gate[None].astype(jnp.bfloat16),
        total_up[None].astype(jnp.bfloat16),
        total_down[None].astype(jnp.bfloat16),
    )


def solution(mesh):
    placed = (
        P("ep", None),
        P("ep", None),
        P("ep", None),
        P("ep", None),
        P(),
        P("ep", None, "rep"),
        P("ep", None, "rep"),
        P("ep", "rep", None),
    )
    return jax.shard_map(
        local,
        mesh=mesh,
        in_specs=placed,
        out_specs=(
            P("ep", None),
            P("ep", None),
            P("ep", None, "rep"),
            P("ep", None, "rep"),
            P("ep", "rep", None),
        ),
        check_vma=False,
    )
```
